256 devices in a mesh: row: 32 (over z, y_hi, core), col: 8 (over y_lo, x).
Axes of the slice: x: 4, y: 4 (y_hi: 2, y_lo: 2; y = y_hi * 2 + y_lo), z: 8, core: 2. Of those that a mesh axis runs over, the one named last changes fastest.
Arguments:
- obs_summaries: bfloat16 [16384, 256], P(('row', 'col')), may hold values from -6 to 6
- sim_summaries: bfloat16 [8192, 256], P('row'), may hold values from -6 to 6
- neighbours: int32 [16384, 16], P(('row', 'col')), may hold values from 0 to 8191
- field: bfloat16 [8192, 8192], P('row', 'col'), may hold values from -6 to 6
Outputs:
- posterior: bfloat16 [16384, 8192], P('row', 'col')
The draws below stay inside these ranges and needn't reach their ends.
Inputs may be any that keep to these rules, and one draw needn't show every extreme that they name: `neighbours`: each entry names a row of sim_summaries.
All inputs are finite; a program needn't handle non-finite values.
Results may differ from the reference program's by a relative error of at most 0.005.
Values may be sent and summed in bfloat16 or wider, within the bound.
A program may use at most 128 MiB of HBM per device.

```python
import jax
import jax.numpy as jnp
from jax import lax

DS = 256
KNN = 16
OBS_DEV = 512
SIM_DEV = 256
NOBS = 16384
NSIM = 8192
NCELL = 8192
N_ROW = 32


def touch_ends(drawn, stream_key, smallest, largest):
    longest = drawn.shape.index(max(drawn.shape))
    spots = []
    for shift in (0, 1):
        where = [jax.random.randint(jax.random.fold_in(stream_key, axis), (), 0, length) for axis, length in enumerate(drawn.shape)]
        where[longest] = (where[longest] + shift) % drawn.shape[longest]
        spots.append(tuple(where))
    return drawn.at[spots[0]].set(smallest).at[spots[1]].set(largest)


def block_levels(stream_key, dims, cuts, least, largest):
    def one(dim, blocks):
        draws = jax.random.uniform(jax.random.fold_in(jax.random.fold_in(stream_key, 6), dim), (blocks,), jnp.float32, least / len(cuts), largest / len(cuts))
        return jnp.repeat(jnp.exp(draws), dims[dim] // blocks).reshape((-1,) + (1,) * (len(dims) - dim - 1))

    loudness = one(*cuts[0])
    for cut in cuts[1:]:
        loudness = loudness * one(*cut)
    return loudness


def scatter_about(rng, extent, spread, reach, shards=(), kind=jnp.bfloat16):
    entries = spread * jax.random.normal(rng, extent, jnp.float32)
    if shards:
        entries = entries * block_levels(rng, extent, shards, -0.22, 0.18)
    return jnp.clip(entries, -reach, reach).astype(kind)


def setup_inputs(seed: int = 0) -> dict:
    keys = jax.random.split(jax.random.key(seed), 5)
    return {
        "obs_summaries": scatter_about(keys[0], (NOBS, DS), 1.0, 6.0, ((0, 256),)),
        "sim_summaries": scatter_about(keys[1], (NSIM, DS), 1.0, 6.0, ((0, 32),)),
        "neighbours": touch_ends(jax.random.randint(keys[2], (NOBS, KNN), 0, NSIM), jax.random.fold_in(keys[2], 1), 0, NSIM - 1).astype(jnp.int32),
        "field": scatter_about(keys[3], (NSIM, NCELL), 1.0, 6.0, ((0, 32), (1, 8))),
    }


SHARPNESS = 32.0
EPSILON = 1e-6


def neighbour_widths(obs_rows, index_rows, sims_full, sim_square):
    obs_float = obs_rows.astype(jnp.float32)
    near_rows = sims_full[index_rows].astype(jnp.float32)
    inner_prod = jnp.einsum("rd,rkd->rk", obs_float, near_rows)
    obs_square = jnp.sum(obs_float * obs_float, axis=1)
    distance = obs_square[:, None] + sim_square[index_rows] - 2.0 * inner_prod
    return jnp.mean(distance, axis=1) + EPSILON


def reference(obs_summaries, sim_summaries, neighbours, field):
    sim_float = sim_summaries.astype(jnp.float32)
    sim_square = jnp.sum(sim_float * sim_float, axis=1)
    obs_blocks = obs_summaries.reshape(N_ROW, OBS_DEV, DS)
    index_blocks = neighbours.reshape(N_ROW, OBS_DEV, KNN)
    sim_blocks = sim_summaries.reshape(N_ROW, SIM_DEV, DS)
    square_blocks = sim_square.reshape(N_ROW, SIM_DEV)
    field_blocks = field.reshape(N_ROW, SIM_DEV, NCELL)

    def one_block(inputs):
        obs_rows, index_rows = inputs
        width = neighbour_widths(obs_rows, index_rows, sim_summaries, sim_square)
        obs_float = obs_rows.astype(jnp.float32)
        obs_square = jnp.sum(obs_float * obs_float, axis=1)

        def step_sims(carry, pieces):
            numer, total = carry
            sim_piece, square_piece, field_piece = pieces
            distance = obs_square[:, None] + square_piece[None, :] - 2.0 * jnp.dot(obs_rows, sim_piece.T, preferred_element_type=jnp.float32)
            weight = jnp.exp(-SHARPNESS * distance / width[:, None])
            numer = numer + jnp.dot(weight.astype(jnp.bfloat16), field_piece, preferred_element_type=jnp.float32)
            total = total + jnp.sum(weight, axis=1)
            return (numer, total), None

        start = (jnp.zeros((OBS_DEV, NCELL), jnp.float32), jnp.zeros((OBS_DEV,), jnp.float32))
        (numer, total), _ = lax.scan(step_sims, start, (sim_blocks, square_blocks, field_blocks))
        return (numer / total[:, None]).astype(jnp.bfloat16)

    result = lax.map(one_block, (obs_blocks, index_blocks))
    return result.reshape(NOBS, NCELL)
```

```python
import jax
import jax.numpy as jnp
import numpy as np
from jax import lax
from jax.sharding import Mesh
from jax.sharding import PartitionSpec as P

SHARPNESS = 32.0
EPSILON = 1e-06
ROWS = ("z", "yh", "core")
COLS = ("yl", "x")


def per_device(obs_summaries, sim_summaries, neighbours, field):
    sim_dev = sim_summaries.shape[0]
    n_chip = lax.psum(1, ("z", "yh"))
    sims_chip = lax.all_gather(sim_summaries, ("z", "yh"), axis=0, tiled=True)
    sims_full = lax.all_gather(sims_chip, "core", axis=0, tiled=True)
    field_chip = lax.all_gather(field, ("z", "yh"), axis=0, tiled=True)
    field_full = lax.all_gather(field_chip, "core", axis=0, tiled=True)
    obs_block = lax.all_gather(obs_summaries, COLS, axis=0, tiled=True)
    index_block = lax.all_gather(neighbours, COLS, axis=0, tiled=True)

    sim_float = sims_full.astype(jnp.float32)
    sim_square = jnp.sum(sim_float * sim_float, axis=1)
    obs_float = obs_block.astype(jnp.float32)
    obs_square = jnp.sum(obs_float * obs_float, axis=1)
    cross = lax.dot_general(
        obs_block, sims_full, (((1,), (1,)), ((), ())), preferred_element_type=jnp.float32
    )
    distance = obs_square[:, None] + sim_square[None, :] - 2.0 * cross

    within = index_block % sim_dev
    owner = index_block // sim_dev
    place = (owner % 2) * (n_chip * sim_dev) + (owner // 2) * sim_dev + within
    near = jnp.take_along_axis(distance, place, axis=1)
    width = jnp.mean(near, axis=1) + EPSILON

    weight = jnp.exp(-SHARPNESS * distance / width[:, None])
    numer = jnp.dot(weight.astype(jnp.bfloat16), field_full, preferred_element_type=jnp.float32)
    total = jnp.sum(weight, axis=1)
    return (numer / total[:, None]).astype(jnp.bfloat16)


def solution(mesh):
    n_row, n_col = mesh.devices.shape
    fine = Mesh(mesh.devices.reshape(n_row // 4, 2, 2, 2, n_col // 2), ROWS + COLS)
    return jax.shard_map(
        per_device,
        mesh=fine,
        in_specs=(
            P(ROWS + COLS, None),
            P(ROWS, None),
            P(ROWS + COLS, None),
            P(ROWS, COLS),
        ),
        out_specs=P(ROWS, COLS),
        check_vma=False,
    )
```

```python
import functools

import jax
import jax.numpy as jnp
from jax import lax
from jax.experimental import pallas as pl
from jax.experimental.pallas import tpu as pltpu
from jax.sharding import Mesh
from jax.sharding import PartitionSpec as P

SHARPNESS = 32.0
EPSILON = 1e-06
ROWS = ("z", "yh", "core")
COLS = ("yl", "x")
MESH = pl.DeviceIdType.MESH


def ring_device(pos, n_z, lane):
    chip = pos // 2
    core = pos % 2
    start = lane * (n_z // 2)
    low = chip < n_z
    z = jnp.where(low, (start + chip) % n_z, (start + 2 * n_z - 1 - chip) % n_z)
    yh = jnp.where(low, 0, 1)
    return z, yh, core


def ring_gather_kernel(n_z, field_ref, sims_ref, field_out, sims_out, send_sem, recv_sem, local_sem):
    z = lax.axis_index("z")
    yh = lax.axis_index("yh")
    core = lax.axis_index("core")
    yl = lax.axis_index("yl")
    x = lax.axis_index("x")
    n = 4 * n_z
    start = yl * (n_z // 2)
    rel = (z - start + n_z) % n_z
    chip = jnp.where(yh == 0, rel, 2 * n_z - 1 - rel)
    pos = 2 * chip + core
    me = (z * 2 + yh) * 2 + core

    def dev(p):
        dz, dyh, dcore = ring_device(p, n_z, yl)
        return (dz, dyh, dcore, yl, x)

    def origin(p):
        dz, dyh, dcore = ring_device(p, n_z, yl)
        return (dz * 2 + dyh) * 2 + dcore

    right = dev((pos + 1) % n)
    left = dev((pos + n - 1) % n)

    barrier = pltpu.get_barrier_semaphore()
    pl.semaphore_signal(barrier, inc=1, device_id=left, device_id_type=MESH)
    pl.semaphore_signal(barrier, inc=1, device_id=right, device_id_type=MESH)
    pl.semaphore_wait(barrier, 2)

    local = [
        pltpu.make_async_copy(field_ref, field_out.at[me], local_sem.at[0]),
        pltpu.make_async_copy(sims_ref, sims_out.at[me], local_sem.at[1]),
    ]
    for c in local:
        c.start()

    n_fwd = n // 2
    n_bwd = n - 1 - n_fwd
    copies = []

    def hop(direction, step, target):
        if direction == 0:
            src_pos = (pos - step + 1 + n) % n
        else:
            src_pos = (pos + step - 1) % n
        o = origin(src_pos)
        made = []
        for k, (src_in, out) in enumerate(((field_ref, field_out), (sims_ref, sims_out))):
            src = src_in if step == 1 else out.at[o]
            made.append(
                pltpu.make_async_remote_copy(
                    src_ref=src,
                    dst_ref=out.at[o],
                    send_sem=send_sem.at[direction, k, step - 1],
                    recv_sem=recv_sem.at[direction, k, step - 1],
                    device_id=target,
                    device_id_type=MESH,
                )
            )
        return made

    prev = {0: None, 1: None}
    for step in range(1, n_fwd + 1):
        for direction, count, target in ((0, n_fwd, right), (1, n_bwd, left)):
            if step > count:
                continue
            if prev[direction] is not None:
                for c in prev[direction]:
                    c.wait_recv()
            made = hop(direction, step, target)
            for c in made:
                c.start()
            copies.extend(made)
            prev[direction] = made
    for direction in (0, 1):
        for c in prev[direction]:
            c.wait_recv()
    for c in copies:
        c.wait_send()
    for c in local:
        c.wait()


def ring_gather(field, sims, n_z):
    n = 4 * n_z
    n_fwd = n // 2
    return pl.pallas_call(
        functools.partial(ring_gather_kernel, n_z),
        out_shape=(
            jax.ShapeDtypeStruct((n,) + field.shape, field.dtype),
            jax.ShapeDtypeStruct((n,) + sims.shape, sims.dtype),
        ),
        in_specs=[pl.BlockSpec(memory_space=pl.ANY)] * 2,
        out_specs=(pl.BlockSpec(memory_space=pl.ANY), pl.BlockSpec(memory_space=pl.ANY)),
        scratch_shapes=[
            pltpu.SemaphoreType.DMA((2, 2, n_fwd)),
            pltpu.SemaphoreType.DMA((2, 2, n_fwd)),
            pltpu.SemaphoreType.DMA((2,)),
        ],
        compiler_params=pltpu.CompilerParams(collective_id=0, has_side_effects=True),
    )(field, sims)


def per_device(n_z, obs_summaries, sim_summaries, neighbours, field):
    field_all, sims_all = ring_gather(field, sim_summaries, n_z)
    field_full = field_all.reshape(-1, field.shape[1])
    sims_full = sims_all.reshape(-1, sim_summaries.shape[1])
    obs_block = lax.all_gather(obs_summaries, COLS, axis=0, tiled=True)
    index_block = lax.all_gather(neighbours, COLS, axis=0, tiled=True)

    sim_float = sims_full.astype(jnp.float32)
    sim_square = jnp.sum(sim_float * sim_float, axis=1)
    obs_float = obs_block.astype(jnp.float32)
    obs_square = jnp.sum(obs_float * obs_float, axis=1)
    cross = lax.dot_general(
        obs_block, sims_full, (((1,), (1,)), ((), ())), preferred_element_type=jnp.float32
    )
    distance = obs_square[:, None] + sim_square[None, :] - 2.0 * cross

    sim_ids = lax.broadcasted_iota(jnp.int32, (1, 1, sims_full.shape[0]), 2)
    counts = jnp.sum((index_block[:, :, None] == sim_ids).astype(jnp.float32), axis=1)
    width = jnp.sum(counts * distance, axis=1) / index_block.shape[1] + EPSILON

    weight = jnp.exp(-SHARPNESS * distance / width[:, None])
    numer = jnp.dot(weight.astype(jnp.bfloat16), field_full, preferred_element_type=jnp.float32)
    total = jnp.sum(weight, axis=1)
    return (numer / total[:, None]).astype(jnp.bfloat16)


def solution(mesh):
    n_row, n_col = mesh.devices.shape
    n_z = n_row // 4
    fine = Mesh(mesh.devices.reshape(n_z, 2, 2, 2, n_col // 2), ROWS + COLS)
    return jax.shard_map(
        functools.partial(per_device, n_z),
        mesh=fine,
        in_specs=(
            P(ROWS + COLS, None),
            P(ROWS, None),
            P(ROWS + COLS, None),
            P(ROWS, COLS),
        ),
        out_specs=P(ROWS, COLS),
        check_vma=False,
    )
```

```python
import functools

import jax
import jax.numpy as jnp
from jax import lax
from jax.experimental import pallas as pl
from jax.experimental.pallas import tpu as pltpu
from jax.sharding import Mesh
from jax.sharding import PartitionSpec as P

SHARPNESS = 32.0
EPSILON = 1e-06
ROWS = ("z", "yh", "core")
COLS = ("yl", "x")
MESH = pl.DeviceIdType.MESH


def ring_device(pos, n_z, lane):
    chip = pos // 2
    core = pos % 2
    start = lane * (n_z // 2)
    low = chip < n_z
    z = jnp.where(low, (start + chip) % n_z, (start + 2 * n_z - 1 - chip) % n_z)
    yh = jnp.where(low, 0, 1)
    return z, yh, core


def col_peers(n_x, yl, x):
    me = yl * n_x + x
    return me, [((me + d) % (2 * n_x)) for d in range(1, 2 * n_x)]


def ring_gather_kernel(
    n_z, field_ref, sims_ref, obs_ref, nbr_ref, field_out, sims_out, obs_out, nbr_out,
    send_sem, recv_sem, local_sem, col_send, col_recv,
):
    z = lax.axis_index("z")
    yh = lax.axis_index("yh")
    core = lax.axis_index("core")
    yl = lax.axis_index("yl")
    x = lax.axis_index("x")
    n = 4 * n_z
    start = yl * (n_z // 2)
    rel = (z - start + n_z) % n_z
    chip = jnp.where(yh == 0, rel, 2 * n_z - 1 - rel)
    pos = 2 * chip + core
    me = (z * 2 + yh) * 2 + core

    def dev(p):
        dz, dyh, dcore = ring_device(p, n_z, yl)
        return (dz, dyh, dcore, yl, x)

    def origin(p):
        dz, dyh, dcore = ring_device(p, n_z, yl)
        return (dz * 2 + dyh) * 2 + dcore

    right = dev((pos + 1) % n)
    left = dev((pos + n - 1) % n)

    n_x = obs_out.shape[0] // 2
    mine, peers = col_peers(n_x, yl, x)
    peer_devs = [(z, yh, core, p // n_x, p % n_x) for p in peers]

    barrier = pltpu.get_barrier_semaphore()
    for d in [left, right] + peer_devs:
        pl.semaphore_signal(barrier, inc=1, device_id=d, device_id_type=MESH)
    pl.semaphore_wait(barrier, 2 + len(peer_devs))

    local = [
        pltpu.make_async_copy(field_ref, field_out.at[me], local_sem.at[0]),
        pltpu.make_async_copy(sims_ref, sims_out.at[me], local_sem.at[1]),
        pltpu.make_async_copy(obs_ref, obs_out.at[mine], local_sem.at[2]),
        pltpu.make_async_copy(nbr_ref, nbr_out.at[mine], local_sem.at[3]),
    ]
    for c in local:
        c.start()
    col_copies = []
    for i, d in enumerate(peer_devs):
        for k, (src, out) in enumerate(((obs_ref, obs_out), (nbr_ref, nbr_out))):
            col_copies.append(
                pltpu.make_async_remote_copy(
                    src_ref=src,
                    dst_ref=out.at[mine],
                    send_sem=col_send.at[k, i],
                    recv_sem=col_recv.at[k, mine],
                    device_id=d,
                    device_id_type=MESH,
                )
            )
    for c in col_copies:
        c.start()

    n_fwd = n // 2
    n_bwd = n - 1 - n_fwd
    copies = []

    def hop(direction, step, target):
        if direction == 0:
            src_pos = (pos - step + 1 + n) % n
        else:
            src_pos = (pos + step - 1) % n
        o = origin(src_pos)
        made = []
        for k, (src_in, out) in enumerate(((field_ref, field_out), (sims_ref, sims_out))):
            src = src_in if step == 1 else out.at[o]
            made.append(
                pltpu.make_async_remote_copy(
                    src_ref=src,
                    dst_ref=out.at[o],
                    send_sem=send_sem.at[direction, k, step - 1],
                    recv_sem=recv_sem.at[direction, k, step - 1],
                    device_id=target,
                    device_id_type=MESH,
                )
            )
        return made

    prev = {0: None, 1: None}
    for step in range(1, n_fwd + 1):
        for direction, count, target in ((0, n_fwd, right), (1, n_bwd, left)):
            if step > count:
                continue
            if prev[direction] is not None:
                for c in prev[direction]:
                    c.wait_recv()
            made = hop(direction, step, target)
            for c in made:
                c.start()
            copies.extend(made)
            prev[direction] = made
    for direction in (0, 1):
        for c in prev[direction]:
            c.wait_recv()
    for p in peers:
        for k, out in enumerate((obs_out, nbr_out)):
            pltpu.make_async_remote_copy(
                src_ref=out.at[p],
                dst_ref=out.at[p],
                send_sem=col_send.at[k, 0],
                recv_sem=col_recv.at[k, p],
                device_id=peer_devs[0],
                device_id_type=MESH,
            ).wait_recv()
    for c in copies + col_copies:
        c.wait_send()
    for c in local:
        c.wait()


def ring_gather(field, sims, obs, nbr, n_z, n_col):
    n = 4 * n_z
    n_fwd = n // 2
    return pl.pallas_call(
        functools.partial(ring_gather_kernel, n_z),
        out_shape=(
            jax.ShapeDtypeStruct((n,) + field.shape, field.dtype),
            jax.ShapeDtypeStruct((n,) + sims.shape, sims.dtype),
            jax.ShapeDtypeStruct((n_col,) + obs.shape, obs.dtype),
            jax.ShapeDtypeStruct((n_col,) + nbr.shape, nbr.dtype),
        ),
        in_specs=[pl.BlockSpec(memory_space=pl.ANY)] * 4,
        out_specs=tuple(pl.BlockSpec(memory_space=pl.ANY) for _ in range(4)),
        scratch_shapes=[
            pltpu.SemaphoreType.DMA((2, 2, n_fwd)),
            pltpu.SemaphoreType.DMA((2, 2, n_fwd)),
            pltpu.SemaphoreType.DMA((4,)),
            pltpu.SemaphoreType.DMA((2, n_col - 1)),
            pltpu.SemaphoreType.DMA((2, n_col)),
        ],
        compiler_params=pltpu.CompilerParams(collective_id=0, has_side_effects=True),
    )(field, sims, obs, nbr)


def col_gather_kernel(val_ref, out_ref, send_sem, recv_sem, local_sem):
    z = lax.axis_index("z")
    yh = lax.axis_index("yh")
    core = lax.axis_index("core")
    yl = lax.axis_index("yl")
    x = lax.axis_index("x")
    n_x = out_ref.shape[0] // 2
    mine, peers = col_peers(n_x, yl, x)
    peer_devs = [(z, yh, core, p // n_x, p % n_x) for p in peers]
    barrier = pltpu.get_barrier_semaphore()
    for d in peer_devs:
        pl.semaphore_signal(barrier, inc=1, device_id=d, device_id_type=MESH)
    pl.semaphore_wait(barrier, len(peer_devs))
    local = pltpu.make_async_copy(val_ref, out_ref.at[mine], local_sem.at[0])
    local.start()
    sent = []
    for i, d in enumerate(peer_devs):
        c = pltpu.make_async_remote_copy(
            src_ref=val_ref,
            dst_ref=out_ref.at[mine],
            send_sem=send_sem.at[i],
            recv_sem=recv_sem.at[mine],
            device_id=d,
            device_id_type=MESH,
        )
        c.start()
        sent.append(c)
    for p in peers:
        pltpu.make_async_remote_copy(
            src_ref=out_ref.at[p],
            dst_ref=out_ref.at[p],
            send_sem=send_sem.at[0],
            recv_sem=recv_sem.at[p],
            device_id=peer_devs[0],
            device_id_type=MESH,
        ).wait_recv()
    for c in sent:
        c.wait_send()
    local.wait()


def col_gather(val, n_col):
    return pl.pallas_call(
        col_gather_kernel,
        out_shape=jax.ShapeDtypeStruct((n_col,) + val.shape, val.dtype),
        in_specs=[pl.BlockSpec(memory_space=pl.ANY)],
        out_specs=pl.BlockSpec(memory_space=pl.ANY),
        scratch_shapes=[
            pltpu.SemaphoreType.DMA((n_col - 1,)),
            pltpu.SemaphoreType.DMA((n_col,)),
            pltpu.SemaphoreType.DMA((1,)),
        ],
        compiler_params=pltpu.CompilerParams(collective_id=1, has_side_effects=True),
    )(val)


def neighbour_widths(obs_rows, index_rows, sims_full):
    obs_float = obs_rows.astype(jnp.float32)
    near_rows = jnp.take(sims_full, index_rows, axis=0).astype(jnp.float32)
    inner_prod = jnp.einsum("rd,rkd->rk", obs_float, near_rows)
    obs_square = jnp.sum(obs_float * obs_float, axis=1)
    near_square = jnp.sum(near_rows * near_rows, axis=2)
    distance = obs_square[:, None] + near_square - 2.0 * inner_prod
    return jnp.mean(distance, axis=1) + EPSILON


def per_device(n_z, obs_summaries, sim_summaries, neighbours, field):
    n_col = 2 * lax.psum(1, "x")
    field_all, sims_all, obs_all, _ = ring_gather(field, sim_summaries, obs_summaries, neighbours, n_z, n_col)
    field_full = field_all.reshape(-1, field.shape[1])
    sims_full = sims_all.reshape(-1, sim_summaries.shape[1])
    obs_block = obs_all.reshape(-1, obs_summaries.shape[1])

    own_width = neighbour_widths(obs_summaries, neighbours, sims_full)
    width = col_gather(own_width.reshape(1, -1), n_col).reshape(-1)

    sim_float = sims_full.astype(jnp.float32)
    sim_square = jnp.sum(sim_float * sim_float, axis=1)
    obs_float = obs_block.astype(jnp.float32)
    obs_square = jnp.sum(obs_float * obs_float, axis=1)
    cross = lax.dot_general(
        obs_block, sims_full, (((1,), (1,)), ((), ())), preferred_element_type=jnp.float32
    )
    distance = obs_square[:, None] + sim_square[None, :] - 2.0 * cross

    weight = jnp.exp(-SHARPNESS * distance / width[:, None])
    numer = jnp.dot(weight.astype(jnp.bfloat16), field_full, preferred_element_type=jnp.float32)
    total = jnp.sum(weight, axis=1)
    return (numer / total[:, None]).astype(jnp.bfloat16)


def solution(mesh):
    n_row, n_col = mesh.devices.shape
    n_z = n_row // 4
    fine = Mesh(mesh.devices.reshape(n_z, 2, 2, 2, n_col // 2), ROWS + COLS)
    return jax.shard_map(
        functools.partial(per_device, n_z),
        mesh=fine,
        in_specs=(
            P(ROWS + COLS, None),
            P(ROWS, None),
            P(ROWS + COLS, None),
            P(ROWS, COLS),
        ),
        out_specs=P(ROWS, COLS),
        check_vma=False,
    )
```

```python
import functools

import jax
import jax.numpy as jnp
from jax import lax
from jax.experimental import pallas as pl
from jax.experimental.pallas import tpu as pltpu
from jax.sharding import Mesh
from jax.sharding import PartitionSpec as P

SHARPNESS = 32.0
EPSILON = 1e-06
ROWS = ("z", "yh", "core")
COLS = ("yl", "x")
MESH = pl.DeviceIdType.MESH


def ring_device(pos, n_z, lane):
    chip = pos // 2
    core = pos % 2
    start = lane * (n_z // 2)
    low = chip < n_z
    z = jnp.where(low, (start + chip) % n_z, (start + 2 * n_z - 1 - chip) % n_z)
    yh = jnp.where(low, 0, 1)
    return z, yh, core


def col_peers(n_x, yl, x):
    me = yl * n_x + x
    return me, [((me + d) % (2 * n_x)) for d in range(1, 2 * n_x)]


def ring_gather_kernel(
    n_z, field_ref, sims_ref, obs_ref, nbr_ref, field_out, sims_out, obs_out, nbr_out,
    send_sem, recv_sem, local_sem, col_send, col_recv, fan_send, fan_recv,
):
    z = lax.axis_index("z")
    yh = lax.axis_index("yh")
    core = lax.axis_index("core")
    yl = lax.axis_index("yl")
    x = lax.axis_index("x")
    n = 4 * n_z
    start = yl * (n_z // 2)
    rel = (z - start + n_z) % n_z
    chip = jnp.where(yh == 0, rel, 2 * n_z - 1 - rel)
    pos = 2 * chip + core
    me = (z * 2 + yh) * 2 + core

    def dev(p):
        dz, dyh, dcore = ring_device(p, n_z, yl)
        return (dz, dyh, dcore, yl, x)

    def origin(p):
        dz, dyh, dcore = ring_device(p, n_z, yl)
        return (dz * 2 + dyh) * 2 + dcore

    right = dev((pos + 1) % n)
    left = dev((pos + n - 1) % n)

    n_x = obs_out.shape[0] // 2
    mine, peers = col_peers(n_x, yl, x)
    peer_devs = [(z, yh, core, p // n_x, p % n_x) for p in peers]

    barrier = pltpu.get_barrier_semaphore()
    for d in [left, right] + peer_devs:
        pl.semaphore_signal(barrier, inc=1, device_id=d, device_id_type=MESH)
    pl.semaphore_wait(barrier, 2 + len(peer_devs))

    local = [
        pltpu.make_async_copy(field_ref, field_out.at[me], local_sem.at[0]),
        pltpu.make_async_copy(sims_ref, sims_out.at[me], local_sem.at[1]),
        pltpu.make_async_copy(obs_ref, obs_out.at[mine], local_sem.at[2]),
        pltpu.make_async_copy(nbr_ref, nbr_out.at[mine], local_sem.at[3]),
    ]
    for c in local:
        c.start()
    col_copies = []
    for i, d in enumerate(peer_devs):
        for k, (src, out) in enumerate(((obs_ref, obs_out), (nbr_ref, nbr_out))):
            col_copies.append(
                pltpu.make_async_remote_copy(
                    src_ref=src,
                    dst_ref=out.at[mine],
                    send_sem=col_send.at[k, i],
                    recv_sem=col_recv.at[k, mine],
                    device_id=d,
                    device_id_type=MESH,
                )
            )
    for c in col_copies:
        c.start()

    n_fwd = n // 2
    n_bwd = n - 1 - n_fwd
    copies = []
    part = sims_ref.shape[0] // (2 * n_x)
    mine_rows = pl.ds(mine * part, part)

    def fan_out(direction, step):
        if direction == 0:
            o = origin((pos - step + n) % n)
        else:
            o = origin((pos + step) % n)
        for i, d in enumerate(peer_devs):
            c = pltpu.make_async_remote_copy(
                src_ref=sims_out.at[o, mine_rows],
                dst_ref=sims_out.at[o, mine_rows],
                send_sem=fan_send.at[direction, step - 1, i],
                recv_sem=fan_recv.at[direction, step - 1, mine],
                device_id=d,
                device_id_type=MESH,
            )
            c.start()
            copies.append(c)

    def hop(direction, step, target):
        if direction == 0:
            src_pos = (pos - step + 1 + n) % n
        else:
            src_pos = (pos + step - 1) % n
        o = origin(src_pos)
        made = []
        for k, (src_in, out) in enumerate(((field_ref, field_out), (sims_ref.at[mine_rows], sims_out))):
            dst = out.at[o] if k == 0 else out.at[o, mine_rows]
            src = src_in if step == 1 else dst
            made.append(
                pltpu.make_async_remote_copy(
                    src_ref=src,
                    dst_ref=dst,
                    send_sem=send_sem.at[direction, k, step - 1],
                    recv_sem=recv_sem.at[direction, k, step - 1],
                    device_id=target,
                    device_id_type=MESH,
                )
            )
        return made

    prev = {0: None, 1: None}
    for step in range(1, n_fwd + 1):
        for direction, count, target in ((0, n_fwd, right), (1, n_bwd, left)):
            if step > count:
                continue
            if prev[direction] is not None:
                for c in prev[direction]:
                    c.wait_recv()
                fan_out(direction, step - 1)
            made = hop(direction, step, target)
            for c in made:
                c.start()
            copies.extend(made)
            prev[direction] = made
    for direction, count in ((0, n_fwd), (1, n_bwd)):
        for c in prev[direction]:
            c.wait_recv()
        fan_out(direction, count)
    for direction, count in ((0, n_fwd), (1, n_bwd)):
        for step in range(1, count + 1):
            for p in peers:
                pltpu.make_async_remote_copy(
                    src_ref=sims_out.at[0, mine_rows],
                    dst_ref=sims_out.at[0, pl.ds(p * part, part)],
                    send_sem=fan_send.at[direction, step - 1, 0],
                    recv_sem=fan_recv.at[direction, step - 1, p],
                    device_id=peer_devs[0],
                    device_id_type=MESH,
                ).wait_recv()
    for p in peers:
        for k, out in enumerate((obs_out, nbr_out)):
            pltpu.make_async_remote_copy(
                src_ref=out.at[p],
                dst_ref=out.at[p],
                send_sem=col_send.at[k, 0],
                recv_sem=col_recv.at[k, p],
                device_id=peer_devs[0],
                device_id_type=MESH,
            ).wait_recv()
    for c in copies + col_copies:
        c.wait_send()
    for c in local:
        c.wait()


def ring_gather(field, sims, obs, nbr, n_z, n_col):
    n = 4 * n_z
    n_fwd = n // 2
    return pl.pallas_call(
        functools.partial(ring_gather_kernel, n_z),
        out_shape=(
            jax.ShapeDtypeStruct((n,) + field.shape, field.dtype),
            jax.ShapeDtypeStruct((n,) + sims.shape, sims.dtype),
            jax.ShapeDtypeStruct((n_col,) + obs.shape, obs.dtype),
            jax.ShapeDtypeStruct((n_col,) + nbr.shape, nbr.dtype),
        ),
        in_specs=[pl.BlockSpec(memory_space=pl.ANY)] * 4,
        out_specs=tuple(pl.BlockSpec(memory_space=pl.ANY) for _ in range(4)),
        scratch_shapes=[
            pltpu.SemaphoreType.DMA((2, 2, n_fwd)),
            pltpu.SemaphoreType.DMA((2, 2, n_fwd)),
            pltpu.SemaphoreType.DMA((4,)),
            pltpu.SemaphoreType.DMA((2, n_col - 1)),
            pltpu.SemaphoreType.DMA((2, n_col)),
            pltpu.SemaphoreType.DMA((2, n_fwd, n_col - 1)),
            pltpu.SemaphoreType.DMA((2, n_fwd, n_col)),
        ],
        compiler_params=pltpu.CompilerParams(collective_id=0, has_side_effects=True),
    )(field, sims, obs, nbr)


def col_gather_kernel(val_ref, out_ref, send_sem, recv_sem, local_sem):
    z = lax.axis_index("z")
    yh = lax.axis_index("yh")
    core = lax.axis_index("core")
    yl = lax.axis_index("yl")
    x = lax.axis_index("x")
    n_x = out_ref.shape[0] // 2
    mine, peers = col_peers(n_x, yl, x)
    peer_devs = [(z, yh, core, p // n_x, p % n_x) for p in peers]
    barrier = pltpu.get_barrier_semaphore()
    for d in peer_devs:
        pl.semaphore_signal(barrier, inc=1, device_id=d, device_id_type=MESH)
    pl.semaphore_wait(barrier, len(peer_devs))
    local = pltpu.make_async_copy(val_ref, out_ref.at[mine], local_sem.at[0])
    local.start()
    sent = []
    for i, d in enumerate(peer_devs):
        c = pltpu.make_async_remote_copy(
            src_ref=val_ref,
            dst_ref=out_ref.at[mine],
            send_sem=send_sem.at[i],
            recv_sem=recv_sem.at[mine],
            device_id=d,
            device_id_type=MESH,
        )
        c.start()
        sent.append(c)
    for p in peers:
        pltpu.make_async_remote_copy(
            src_ref=out_ref.at[p],
            dst_ref=out_ref.at[p],
            send_sem=send_sem.at[0],
            recv_sem=recv_sem.at[p],
            device_id=peer_devs[0],
            device_id_type=MESH,
        ).wait_recv()
    for c in sent:
        c.wait_send()
    local.wait()


def col_gather(val, n_col):
    return pl.pallas_call(
        col_gather_kernel,
        out_shape=jax.ShapeDtypeStruct((n_col,) + val.shape, val.dtype),
        in_specs=[pl.BlockSpec(memory_space=pl.ANY)],
        out_specs=pl.BlockSpec(memory_space=pl.ANY),
        scratch_shapes=[
            pltpu.SemaphoreType.DMA((n_col - 1,)),
            pltpu.SemaphoreType.DMA((n_col,)),
            pltpu.SemaphoreType.DMA((1,)),
        ],
        compiler_params=pltpu.CompilerParams(collective_id=1, has_side_effects=True),
    )(val)


def neighbour_widths(obs_rows, index_rows, sims_full):
    obs_float = obs_rows.astype(jnp.float32)
    near_rows = jnp.take(sims_full, index_rows, axis=0).astype(jnp.float32)
    inner_prod = jnp.einsum("rd,rkd->rk", obs_float, near_rows)
    obs_square = jnp.sum(obs_float * obs_float, axis=1)
    near_square = jnp.sum(near_rows * near_rows, axis=2)
    distance = obs_square[:, None] + near_square - 2.0 * inner_prod
    return jnp.mean(distance, axis=1) + EPSILON


def per_device(n_z, obs_summaries, sim_summaries, neighbours, field):
    n_col = 2 * lax.psum(1, "x")
    field_all, sims_all, obs_all, _ = ring_gather(field, sim_summaries, obs_summaries, neighbours, n_z, n_col)
    field_full = field_all.reshape(-1, field.shape[1])
    sims_full = sims_all.reshape(-1, sim_summaries.shape[1])
    obs_block = obs_all.reshape(-1, obs_summaries.shape[1])

    own_width = neighbour_widths(obs_summaries, neighbours, sims_full)
    width = col_gather(own_width.reshape(1, -1), n_col).reshape(-1)

    sim_float = sims_full.astype(jnp.float32)
    sim_square = jnp.sum(sim_float * sim_float, axis=1)
    obs_float = obs_block.astype(jnp.float32)
    obs_square = jnp.sum(obs_float * obs_float, axis=1)
    cross = lax.dot_general(
        obs_block, sims_full, (((1,), (1,)), ((), ())), preferred_element_type=jnp.float32
    )
    distance = obs_square[:, None] + sim_square[None, :] - 2.0 * cross

    weight = jnp.exp(-SHARPNESS * distance / width[:, None])
    numer = jnp.dot(weight.astype(jnp.bfloat16), field_full, preferred_element_type=jnp.float32)
    total = jnp.sum(weight, axis=1)
    return (numer / total[:, None]).astype(jnp.bfloat16)


def solution(mesh):
    n_row, n_col = mesh.devices.shape
    n_z = n_row // 4
    fine = Mesh(mesh.devices.reshape(n_z, 2, 2, 2, n_col // 2), ROWS + COLS)
    return jax.shard_map(
        functools.partial(per_device, n_z),
        mesh=fine,
        in_specs=(
            P(ROWS + COLS, None),
            P(ROWS, None),
            P(ROWS + COLS, None),
            P(ROWS, COLS),
        ),
        out_specs=P(ROWS, COLS),
        check_vma=False,
    )
```

```python
import functools

import jax
import jax.numpy as jnp
from jax import lax
from jax.experimental import pallas as pl
from jax.experimental.pallas import tpu as pltpu
from jax.sharding import Mesh
from jax.sharding import PartitionSpec as P

SHARPNESS = 32.0
EPSILON = 1e-06
ROWS = ("z", "yh", "core")
COLS = ("yl", "x")
MESH = pl.DeviceIdType.MESH


def ring_device(pos, n_z, lane):
    chip = pos // 2
    core = pos % 2
    start = lane * (n_z // 2)
    low = chip < n_z
    z = jnp.where(low, (start + chip) % n_z, (start + 2 * n_z - 1 - chip) % n_z)
    yh = jnp.where(low, 0, 1)
    return z, yh, core


def col_peers(n_x, yl, x):
    me = yl * n_x + x
    return me, [((me + d) % (2 * n_x)) for d in range(1, 2 * n_x)]


def ring_gather_kernel(
    n_z, field_ref, sims_ref, obs_ref, nbr_ref, field_out, sims_out, obs_out, nbr_out,
    send_sem, recv_sem, local_sem, col_send, col_recv, fan_send, fan_recv,
):
    z = lax.axis_index("z")
    yh = lax.axis_index("yh")
    core = lax.axis_index("core")
    yl = lax.axis_index("yl")
    x = lax.axis_index("x")
    n = 4 * n_z
    start = yl * (n_z // 2)
    rel = (z - start + n_z) % n_z
    chip = jnp.where(yh == 0, rel, 2 * n_z - 1 - rel)
    pos = 2 * chip + core
    me = (z * 2 + yh) * 2 + core

    def dev(p):
        dz, dyh, dcore = ring_device(p, n_z, yl)
        return (dz, dyh, dcore, yl, x)

    def origin(p):
        dz, dyh, dcore = ring_device(p, n_z, yl)
        return (dz * 2 + dyh) * 2 + dcore

    right = dev((pos + 1) % n)
    left = dev((pos + n - 1) % n)

    n_x = obs_out.shape[0] // 2
    mine, peers = col_peers(n_x, yl, x)
    peer_devs = [(z, yh, core, p // n_x, p % n_x) for p in peers]

    barrier = pltpu.get_barrier_semaphore()
    for d in [left, right] + peer_devs:
        pl.semaphore_signal(barrier, inc=1, device_id=d, device_id_type=MESH)
    pl.semaphore_wait(barrier, 2 + len(peer_devs))

    local = [
        pltpu.make_async_copy(field_ref, field_out.at[me], local_sem.at[0]),
        pltpu.make_async_copy(sims_ref, sims_out.at[me], local_sem.at[1]),
        pltpu.make_async_copy(obs_ref, obs_out.at[mine], local_sem.at[2]),
        pltpu.make_async_copy(nbr_ref, nbr_out.at[mine], local_sem.at[3]),
    ]
    for c in local:
        c.start()
    col_copies = []
    for i, d in enumerate(peer_devs):
        for k, (src, out) in enumerate(((obs_ref, obs_out), (nbr_ref, nbr_out))):
            col_copies.append(
                pltpu.make_async_remote_copy(
                    src_ref=src,
                    dst_ref=out.at[mine],
                    send_sem=col_send.at[k, i],
                    recv_sem=col_recv.at[k, mine],
                    device_id=d,
                    device_id_type=MESH,
                )
            )
    for c in col_copies:
        c.start()

    n_fwd = n // 2
    n_bwd = n - 1 - n_fwd
    copies = []
    part = sims_ref.shape[0] // (2 * n_x)
    mine_rows = pl.ds(mine * part, part)

    def fan_out(direction, step):
        if direction == 0:
            o = origin((pos - step + n) % n)
        else:
            o = origin((pos + step) % n)
        for i, d in enumerate(peer_devs):
            c = pltpu.make_async_remote_copy(
                src_ref=sims_out.at[o, mine_rows],
                dst_ref=sims_out.at[o, mine_rows],
                send_sem=fan_send.at[direction, step - 1, i],
                recv_sem=fan_recv.at[direction, step - 1, mine],
                device_id=d,
                device_id_type=MESH,
            )
            c.start()
            copies.append(c)

    def hop(direction, step, target):
        if direction == 0:
            src_pos = (pos - step + 1 + n) % n
        else:
            src_pos = (pos + step - 1) % n
        o = origin(src_pos)
        made = []
        for k, (src_in, out) in enumerate(((field_ref, field_out), (sims_ref.at[mine_rows], sims_out))):
            dst = out.at[o] if k == 0 else out.at[o, mine_rows]
            src = src_in if step == 1 else dst
            made.append(
                pltpu.make_async_remote_copy(
                    src_ref=src,
                    dst_ref=dst,
                    send_sem=send_sem.at[direction, k, step - 1],
                    recv_sem=recv_sem.at[direction, k, step - 1],
                    device_id=target,
                    device_id_type=MESH,
                )
            )
        return made

    prev = {0: None, 1: None}
    for step in range(1, n_fwd + 1):
        arrived = []
        for direction, count, target in ((0, n_fwd, right), (1, n_bwd, left)):
            if step > count:
                continue
            if prev[direction] is not None:
                for c in prev[direction]:
                    c.wait_recv()
                arrived.append(direction)
            made = hop(direction, step, target)
            for c in made:
                c.start()
            copies.extend(made)
            prev[direction] = made
        for direction in arrived:
            fan_out(direction, step - 1)
    for direction, count in ((0, n_fwd), (1, n_bwd)):
        for c in prev[direction]:
            c.wait_recv()
        fan_out(direction, count)
    for direction, count in ((0, n_fwd), (1, n_bwd)):
        for step in range(1, count + 1):
            for p in peers:
                pltpu.make_async_remote_copy(
                    src_ref=sims_out.at[0, mine_rows],
                    dst_ref=sims_out.at[0, pl.ds(p * part, part)],
                    send_sem=fan_send.at[direction, step - 1, 0],
                    recv_sem=fan_recv.at[direction, step - 1, p],
                    device_id=peer_devs[0],
                    device_id_type=MESH,
                ).wait_recv()
    for p in peers:
        for k, out in enumerate((obs_out, nbr_out)):
            pltpu.make_async_remote_copy(
                src_ref=out.at[p],
                dst_ref=out.at[p],
                send_sem=col_send.at[k, 0],
                recv_sem=col_recv.at[k, p],
                device_id=peer_devs[0],
                device_id_type=MESH,
            ).wait_recv()
    for c in copies + col_copies:
        c.wait_send()
    for c in local:
        c.wait()


def ring_gather(field, sims, obs, nbr, n_z, n_col):
    n = 4 * n_z
    n_fwd = n // 2
    return pl.pallas_call(
        functools.partial(ring_gather_kernel, n_z),
        out_shape=(
            jax.ShapeDtypeStruct((n,) + field.shape, field.dtype),
            jax.ShapeDtypeStruct((n,) + sims.shape, sims.dtype),
            jax.ShapeDtypeStruct((n_col,) + obs.shape, obs.dtype),
            jax.ShapeDtypeStruct((n_col,) + nbr.shape, nbr.dtype),
        ),
        in_specs=[pl.BlockSpec(memory_space=pl.ANY)] * 4,
        out_specs=tuple(pl.BlockSpec(memory_space=pl.ANY) for _ in range(4)),
        scratch_shapes=[
            pltpu.SemaphoreType.DMA((2, 2, n_fwd)),
            pltpu.SemaphoreType.DMA((2, 2, n_fwd)),
            pltpu.SemaphoreType.DMA((4,)),
            pltpu.SemaphoreType.DMA((2, n_col - 1)),
            pltpu.SemaphoreType.DMA((2, n_col)),
            pltpu.SemaphoreType.DMA((2, n_fwd, n_col - 1)),
            pltpu.SemaphoreType.DMA((2, n_fwd, n_col)),
        ],
        compiler_params=pltpu.CompilerParams(collective_id=0, has_side_effects=True),
    )(field, sims, obs, nbr)


def col_gather_kernel(val_ref, out_ref, send_sem, recv_sem, local_sem):
    z = lax.axis_index("z")
    yh = lax.axis_index("yh")
    core = lax.axis_index("core")
    yl = lax.axis_index("yl")
    x = lax.axis_index("x")
    n_x = out_ref.shape[0] // 2
    mine, peers = col_peers(n_x, yl, x)
    peer_devs = [(z, yh, core, p // n_x, p % n_x) for p in peers]
    barrier = pltpu.get_barrier_semaphore()
    for d in peer_devs:
        pl.semaphore_signal(barrier, inc=1, device_id=d, device_id_type=MESH)
    pl.semaphore_wait(barrier, len(peer_devs))
    local = pltpu.make_async_copy(val_ref, out_ref.at[mine], local_sem.at[0])
    local.start()
    sent = []
    for i, d in enumerate(peer_devs):
        c = pltpu.make_async_remote_copy(
            src_ref=val_ref,
            dst_ref=out_ref.at[mine],
            send_sem=send_sem.at[i],
            recv_sem=recv_sem.at[mine],
            device_id=d,
            device_id_type=MESH,
        )
        c.start()
        sent.append(c)
    for p in peers:
        pltpu.make_async_remote_copy(
            src_ref=out_ref.at[p],
            dst_ref=out_ref.at[p],
            send_sem=send_sem.at[0],
            recv_sem=recv_sem.at[p],
            device_id=peer_devs[0],
            device_id_type=MESH,
        ).wait_recv()
    for c in sent:
        c.wait_send()
    local.wait()


def col_gather(val, n_col):
    return pl.pallas_call(
        col_gather_kernel,
        out_shape=jax.ShapeDtypeStruct((n_col,) + val.shape, val.dtype),
        in_specs=[pl.BlockSpec(memory_space=pl.ANY)],
        out_specs=pl.BlockSpec(memory_space=pl.ANY),
        scratch_shapes=[
            pltpu.SemaphoreType.DMA((n_col - 1,)),
            pltpu.SemaphoreType.DMA((n_col,)),
            pltpu.SemaphoreType.DMA((1,)),
        ],
        compiler_params=pltpu.CompilerParams(collective_id=1, has_side_effects=True),
    )(val)


def neighbour_widths(obs_rows, index_rows, sims_full):
    obs_float = obs_rows.astype(jnp.float32)
    near_rows = jnp.take(sims_full, index_rows, axis=0).astype(jnp.float32)
    inner_prod = jnp.einsum("rd,rkd->rk", obs_float, near_rows)
    obs_square = jnp.sum(obs_float * obs_float, axis=1)
    near_square = jnp.sum(near_rows * near_rows, axis=2)
    distance = obs_square[:, None] + near_square - 2.0 * inner_prod
    return jnp.mean(distance, axis=1) + EPSILON


def per_device(n_z, obs_summaries, sim_summaries, neighbours, field):
    n_col = 2 * lax.psum(1, "x")
    field_all, sims_all, obs_all, _ = ring_gather(field, sim_summaries, obs_summaries, neighbours, n_z, n_col)
    field_full = field_all.reshape(-1, field.shape[1])
    sims_full = sims_all.reshape(-1, sim_summaries.shape[1])
    obs_block = obs_all.reshape(-1, obs_summaries.shape[1])

    own_width = neighbour_widths(obs_summaries, neighbours, sims_full)
    width = col_gather(own_width.reshape(1, -1), n_col).reshape(-1)

    sim_float = sims_full.astype(jnp.float32)
    sim_square = jnp.sum(sim_float * sim_float, axis=1)
    obs_float = obs_block.astype(jnp.float32)
    obs_square = jnp.sum(obs_float * obs_float, axis=1)
    cross = lax.dot_general(
        obs_block, sims_full, (((1,), (1,)), ((), ())), preferred_element_type=jnp.float32
    )
    distance = obs_square[:, None] + sim_square[None, :] - 2.0 * cross

    weight = jnp.exp(-SHARPNESS * distance / width[:, None])
    numer = jnp.dot(weight.astype(jnp.bfloat16), field_full, preferred_element_type=jnp.float32)
    total = jnp.sum(weight, axis=1)
    return (numer / total[:, None]).astype(jnp.bfloat16)


def solution(mesh):
    n_row, n_col = mesh.devices.shape
    n_z = n_row // 4
    fine = Mesh(mesh.devices.reshape(n_z, 2, 2, 2, n_col // 2), ROWS + COLS)
    return jax.shard_map(
        functools.partial(per_device, n_z),
        mesh=fine,
        in_specs=(
            P(ROWS + COLS, None),
            P(ROWS, None),
            P(ROWS + COLS, None),
            P(ROWS, COLS),
        ),
        out_specs=P(ROWS, COLS),
        check_vma=False,
    )
```

```python
import functools

import jax
import jax.numpy as jnp
from jax import lax
from jax.experimental import pallas as pl
from jax.experimental.pallas import tpu as pltpu
from jax.sharding import Mesh
from jax.sharding import PartitionSpec as P

SHARPNESS = 32.0
EPSILON = 1e-06
ROWS = ("z", "yh", "core")
COLS = ("yl", "x")
MESH = pl.DeviceIdType.MESH


def ring_device(pos, n_z, lane):
    chip = pos // 2
    core = pos % 2
    start = lane * (n_z // 2)
    low = chip < n_z
    z = jnp.where(low, (start + chip) % n_z, (start + 2 * n_z - 1 - chip) % n_z)
    yh = jnp.where(low, 0, 1)
    return z, yh, core


def posterior_kernel(
    n_z, field_ref, sims_ref, sq_ref, obs_ref, nbr_ref, out_ref,
    fbuf, sbuf, qbuf, obuf, wbuf, numer, total, ns,
    send_sem, recv_sem, col_send, col_recv, wid_send, wid_recv,
):
    z = lax.axis_index("z")
    yh = lax.axis_index("yh")
    core = lax.axis_index("core")
    yl = lax.axis_index("yl")
    x = lax.axis_index("x")
    n = 4 * n_z
    n_col = obuf.shape[0]
    n_x = n_col // 2
    sim_dev = sims_ref.shape[0]
    start = yl * (n_z // 2)
    rel = (z - start + n_z) % n_z
    chip = jnp.where(yh == 0, rel, 2 * n_z - 1 - rel)
    pos = 2 * chip + core
    me = (z * 2 + yh) * 2 + core
    mine = yl * n_x + x
    peers = [(mine + d) % n_col for d in range(1, n_col)]
    peer_devs = [(z, yh, core, p // n_x, p % n_x) for p in peers]

    def dev(p):
        dz, dyh, dcore = ring_device(p, n_z, yl)
        return (dz, dyh, dcore, yl, x)

    def origin(p):
        dz, dyh, dcore = ring_device(p, n_z, yl)
        return (dz * 2 + dyh) * 2 + dcore

    right = dev((pos + 1) % n)
    left = dev((pos + n - 1) % n)

    barrier = pltpu.get_barrier_semaphore()
    for d in [left, right] + peer_devs:
        pl.semaphore_signal(barrier, inc=1, device_id=d, device_id_type=MESH)
    pl.semaphore_wait(barrier, 2 + len(peer_devs))

    copies = []
    for i, d in enumerate(peer_devs):
        c = pltpu.make_async_remote_copy(
            src_ref=obs_ref, dst_ref=obuf.at[mine], send_sem=col_send.at[i],
            recv_sem=col_recv.at[mine], device_id=d, device_id_type=MESH,
        )
        c.start()
        copies.append(c)

    n_fwd = n // 2
    n_bwd = n - 1 - n_fwd
    pairs = ((field_ref, fbuf), (sims_ref, sbuf), (sq_ref, qbuf))

    def hop(direction, step, target):
        if direction == 0:
            src_pos = (pos - step + 1 + n) % n
        else:
            src_pos = (pos + step - 1) % n
        o = origin(src_pos)
        made = []
        for k, (src_in, buf) in enumerate(pairs):
            src = src_in if step == 1 else buf.at[o]
            made.append(
                pltpu.make_async_remote_copy(
                    src_ref=src, dst_ref=buf.at[o],
                    send_sem=send_sem.at[direction, k, step - 1],
                    recv_sem=recv_sem.at[direction, k, step - 1],
                    device_id=target, device_id_type=MESH,
                )
            )
        return made

    obs_own = obs_ref[...]
    obs_own_f = obs_own.astype(jnp.float32)
    obs_own_sq = jnp.sum(obs_own_f * obs_own_f, axis=1, keepdims=True)
    nbr = nbr_ref[...]
    ns[...] = jnp.zeros_like(ns)

    def neighbour_sums(o, sims_blk, sq_blk):
        cross = lax.dot_general(
            obs_own, sims_blk, (((1,), (1,)), ((), ())), preferred_element_type=jnp.float32
        )
        dist = obs_own_sq + sq_blk - 2.0 * cross
        ids = lax.broadcasted_iota(jnp.int32, dist.shape, 1) + o * sim_dev
        counts = jnp.zeros(dist.shape, jnp.float32)
        for k in range(nbr.shape[1]):
            counts = counts + (nbr[:, k : k + 1] == ids).astype(jnp.float32)
        ns[...] += jnp.sum(counts * dist, axis=1, keepdims=True)

    fbuf[me] = field_ref[...]
    sbuf[me] = sims_ref[...]
    qbuf[me] = sq_ref[...]
    obuf[mine] = obs_own

    prev = {0: None, 1: None}
    for step in range(1, n_fwd + 1):
        arrived = []
        for direction, count, target in ((0, n_fwd, right), (1, n_bwd, left)):
            if step > count:
                continue
            if prev[direction] is not None:
                for c in prev[direction]:
                    c.wait_recv()
                arrived.append(direction)
            made = hop(direction, step, target)
            for c in made:
                c.start()
            copies.extend(made)
            prev[direction] = made
        if step == 1:
            neighbour_sums(me, sims_ref[...], sq_ref[...])
        for direction in arrived:
            got = (pos - step + 1 + n) % n if direction == 0 else (pos + step - 1) % n
            o = origin(got)
            neighbour_sums(o, sbuf[o], qbuf[o])
    for direction, count in ((0, n_fwd), (1, n_bwd)):
        for c in prev[direction]:
            c.wait_recv()
        got = (pos - count + n) % n if direction == 0 else (pos + count) % n
        o = origin(got)
        neighbour_sums(o, sbuf[o], qbuf[o])

    wbuf[mine] = ns[...] / nbr.shape[1] + EPSILON
    wid = []
    for i, d in enumerate(peer_devs):
        c = pltpu.make_async_remote_copy(
            src_ref=wbuf.at[mine], dst_ref=wbuf.at[mine], send_sem=wid_send.at[i],
            recv_sem=wid_recv.at[mine], device_id=d, device_id_type=MESH,
        )
        c.start()
        wid.append(c)
    for p in peers:
        pltpu.make_async_remote_copy(
            src_ref=obuf.at[p], dst_ref=obuf.at[p], send_sem=col_send.at[0],
            recv_sem=col_recv.at[p], device_id=peer_devs[0], device_id_type=MESH,
        ).wait_recv()
        pltpu.make_async_remote_copy(
            src_ref=wbuf.at[p], dst_ref=wbuf.at[p], send_sem=wid_send.at[0],
            recv_sem=wid_recv.at[p], device_id=peer_devs[0], device_id_type=MESH,
        ).wait_recv()
    for c in copies + wid:
        c.wait_send()

    rows = n_col * obs_ref.shape[0]
    obs_all = obuf[...].reshape(rows, obs_ref.shape[1])
    obs_all_f = obs_all.astype(jnp.float32)
    obs_sq = jnp.sum(obs_all_f * obs_all_f, axis=1, keepdims=True)
    width = wbuf[...].reshape(rows, 1)
    numer[...] = jnp.zeros_like(numer)
    total[...] = jnp.zeros_like(total)

    @pl.loop(0, n)
    def _(b):
        cross = lax.dot_general(
            obs_all, sbuf[b], (((1,), (1,)), ((), ())), preferred_element_type=jnp.float32
        )
        dist = obs_sq + qbuf[b] - 2.0 * cross
        weight = jnp.exp(-SHARPNESS * dist / width)
        total[...] += jnp.sum(weight, axis=1, keepdims=True)
        numer[...] += jnp.dot(weight.astype(jnp.bfloat16), fbuf[b], preferred_element_type=jnp.float32)

    out_ref[...] = (numer[...] / total[...]).astype(out_ref.dtype)


def posterior(field, sims, sq, obs, nbr, n_z, n_col):
    n = 4 * n_z
    n_fwd = n // 2
    rows = n_col * obs.shape[0]
    vmem = pltpu.VMEM
    return pl.pallas_call(
        functools.partial(posterior_kernel, n_z),
        out_shape=jax.ShapeDtypeStruct((rows, field.shape[1]), field.dtype),
        in_specs=[pl.BlockSpec(memory_space=vmem)] * 5,
        out_specs=pl.BlockSpec(memory_space=vmem),
        scratch_shapes=[
            vmem((n,) + field.shape, field.dtype),
            vmem((n,) + sims.shape, sims.dtype),
            vmem((n,) + sq.shape, sq.dtype),
            vmem((n_col,) + obs.shape, obs.dtype),
            vmem((n_col, obs.shape[0], 1), jnp.float32),
            vmem((rows, field.shape[1]), jnp.float32),
            vmem((rows, 1), jnp.float32),
            vmem((obs.shape[0], 1), jnp.float32),
            pltpu.SemaphoreType.DMA((2, 3, n_fwd)),
            pltpu.SemaphoreType.DMA((2, 3, n_fwd)),
            pltpu.SemaphoreType.DMA((n_col - 1,)),
            pltpu.SemaphoreType.DMA((n_col,)),
            pltpu.SemaphoreType.DMA((n_col - 1,)),
            pltpu.SemaphoreType.DMA((n_col,)),
        ],
        compiler_params=pltpu.CompilerParams(
            collective_id=0, has_side_effects=True, vmem_limit_bytes=60 * 1024 * 1024
        ),
    )(field, sims, sq, obs, nbr)


def per_device(n_z, obs_summaries, sim_summaries, neighbours, field):
    n_col = 2 * lax.psum(1, "x")
    sim_float = sim_summaries.astype(jnp.float32)
    sim_square = jnp.sum(sim_float * sim_float, axis=1).reshape(1, -1)
    return posterior(field, sim_summaries, sim_square, obs_summaries, neighbours, n_z, n_col)


def solution(mesh):
    n_row, n_col = mesh.devices.shape
    n_z = n_row // 4
    fine = Mesh(mesh.devices.reshape(n_z, 2, 2, 2, n_col // 2), ROWS + COLS)
    return jax.shard_map(
        functools.partial(per_device, n_z),
        mesh=fine,
        in_specs=(
            P(ROWS + COLS, None),
            P(ROWS, None),
            P(ROWS + COLS, None),
            P(ROWS, COLS),
        ),
        out_specs=P(ROWS, COLS),
        check_vma=False,
    )
```

```python
import functools

import jax
import jax.numpy as jnp
from jax import lax
from jax.experimental import pallas as pl
from jax.experimental.pallas import tpu as pltpu
from jax.sharding import Mesh
from jax.sharding import PartitionSpec as P

SHARPNESS = 32.0
EPSILON = 1e-06
ROWS = ("z", "yh", "core")
COLS = ("yl", "x")
MESH = pl.DeviceIdType.MESH


def ring_device(pos, n_z, lane):
    chip = pos // 2
    core = pos % 2
    start = lane * (n_z // 2)
    low = chip < n_z
    z = jnp.where(low, (start + chip) % n_z, (start + 2 * n_z - 1 - chip) % n_z)
    yh = jnp.where(low, 0, 1)
    return z, yh, core


def posterior_kernel(
    n_z, field_ref, sims_ref, sq_ref, obs_ref, nbr_ref, out_ref,
    fbuf, sbuf, qbuf, obuf, wbuf, numer, total, ns, osq, wcol,
    send_sem, recv_sem, col_send, col_recv, wid_send, wid_recv,
):
    z = lax.axis_index("z")
    yh = lax.axis_index("yh")
    core = lax.axis_index("core")
    yl = lax.axis_index("yl")
    x = lax.axis_index("x")
    n = 4 * n_z
    n_col = obuf.shape[0]
    n_x = n_col // 2
    sim_dev = sims_ref.shape[0]
    start = yl * (n_z // 2)
    rel = (z - start + n_z) % n_z
    chip = jnp.where(yh == 0, rel, 2 * n_z - 1 - rel)
    pos = 2 * chip + core
    me = (z * 2 + yh) * 2 + core
    mine = yl * n_x + x
    peers = [(mine + d) % n_col for d in range(1, n_col)]
    peer_devs = [(z, yh, core, p // n_x, p % n_x) for p in peers]

    def dev(p):
        dz, dyh, dcore = ring_device(p, n_z, yl)
        return (dz, dyh, dcore, yl, x)

    def origin(p):
        dz, dyh, dcore = ring_device(p, n_z, yl)
        return (dz * 2 + dyh) * 2 + dcore

    right = dev((pos + 1) % n)
    left = dev((pos + n - 1) % n)

    barrier = pltpu.get_barrier_semaphore()
    for d in [left, right] + peer_devs:
        pl.semaphore_signal(barrier, inc=1, device_id=d, device_id_type=MESH)
    pl.semaphore_wait(barrier, 2 + len(peer_devs))

    copies = []
    for i, d in enumerate(peer_devs):
        c = pltpu.make_async_remote_copy(
            src_ref=obs_ref, dst_ref=obuf.at[mine], send_sem=col_send.at[i],
            recv_sem=col_recv.at[mine], device_id=d, device_id_type=MESH,
        )
        c.start()
        copies.append(c)

    n_fwd = n // 2
    n_bwd = n - 1 - n_fwd
    count = {0: n_fwd, 1: n_bwd}
    target = {0: right, 1: left}
    field_pairs = ((0, field_ref, fbuf),)
    sims_pairs = ((1, sims_ref, sbuf), (2, sq_ref, qbuf))

    def src_pos(direction, step):
        if direction == 0:
            return (pos - step + 1 + n) % n
        return (pos + step - 1) % n

    def hop(pairs, direction, step):
        o = origin(src_pos(direction, step))
        made = []
        for k, src_in, buf in pairs:
            src = src_in if step == 1 else buf.at[o]
            made.append(
                pltpu.make_async_remote_copy(
                    src_ref=src, dst_ref=buf.at[o],
                    send_sem=send_sem.at[direction, k, step - 1],
                    recv_sem=recv_sem.at[direction, k, step - 1],
                    device_id=target[direction], device_id_type=MESH,
                )
            )
        for c in made:
            c.start()
        copies.extend(made)
        return made

    obs_own = obs_ref[...]
    obs_own_f = obs_own.astype(jnp.float32)
    obs_own_sq = jnp.sum(obs_own_f * obs_own_f, axis=1, keepdims=True)
    nbr = nbr_ref[...]
    ns[...] = jnp.zeros_like(ns)

    def neighbour_sums(o, sims_blk, sq_blk):
        cross = lax.dot_general(
            obs_own, sims_blk, (((1,), (1,)), ((), ())), preferred_element_type=jnp.float32
        )
        dist = obs_own_sq + sq_blk - 2.0 * cross
        ids = lax.broadcasted_iota(jnp.int32, dist.shape, 1) + o * sim_dev
        counts = jnp.zeros(dist.shape, jnp.float32)
        for k in range(nbr.shape[1]):
            counts = counts + (nbr[:, k : k + 1] == ids).astype(jnp.float32)
        ns[...] += jnp.sum(counts * dist, axis=1, keepdims=True)

    fbuf[me] = field_ref[...]
    sbuf[me] = sims_ref[...]
    qbuf[me] = sq_ref[...]
    obuf[mine] = obs_own
    numer[...] = jnp.zeros_like(numer)
    total[...] = jnp.zeros_like(total)
    rows = n_col * obs_ref.shape[0]

    state = {"f": {0: 0, 1: 0}, "s": {0: 0, 1: 0}, "pf": {0: None, 1: None}, "ps": {0: None, 1: None}}
    pending = [me]
    wid = []

    def advance(kind, direction):
        step = state[kind][direction] + 1
        if step > count[direction]:
            return
        before = state["p" + kind][direction]
        if before is not None:
            for c in before:
                c.wait_recv()
            o = origin(src_pos(direction, step))
            if kind == "f":
                pending.append(o)
            else:
                neighbour_sums(o, sbuf[o], qbuf[o])
        state["p" + kind][direction] = hop(field_pairs if kind == "f" else sims_pairs, direction, step)
        state[kind][direction] = step

    def finish(kind, direction):
        for c in state["p" + kind][direction]:
            c.wait_recv()
        last = count[direction]
        o = origin((pos - last + n) % n if direction == 0 else (pos + last) % n)
        if kind == "f":
            pending.append(o)
        else:
            neighbour_sums(o, sbuf[o], qbuf[o])

    def share_widths():
        for direction in (0, 1):
            finish("s", direction)
        wbuf[mine] = ns[...] / nbr.shape[1] + EPSILON
        for i, d in enumerate(peer_devs):
            c = pltpu.make_async_remote_copy(
                src_ref=wbuf.at[mine], dst_ref=wbuf.at[mine], send_sem=wid_send.at[i],
                recv_sem=wid_recv.at[mine], device_id=d, device_id_type=MESH,
            )
            c.start()
            wid.append(c)
        for p in peers:
            pltpu.make_async_remote_copy(
                src_ref=obuf.at[p], dst_ref=obuf.at[p], send_sem=col_send.at[0],
                recv_sem=col_recv.at[p], device_id=peer_devs[0], device_id_type=MESH,
            ).wait_recv()
            pltpu.make_async_remote_copy(
                src_ref=wbuf.at[p], dst_ref=wbuf.at[p], send_sem=wid_send.at[0],
                recv_sem=wid_recv.at[p], device_id=peer_devs[0], device_id_type=MESH,
            ).wait_recv()
        obs_all_f = obuf[...].reshape(rows, obs_ref.shape[1]).astype(jnp.float32)
        osq[...] = jnp.sum(obs_all_f * obs_all_f, axis=1, keepdims=True)
        wcol[...] = wbuf[...].reshape(rows, 1)

    def process(b):
        obs_all = obuf[...].reshape(rows, obs_ref.shape[1])
        cross = lax.dot_general(
            obs_all, sbuf[b], (((1,), (1,)), ((), ())), preferred_element_type=jnp.float32
        )
        dist = osq[...] + qbuf[b] - 2.0 * cross
        weight = jnp.exp(-SHARPNESS * dist / wcol[...])
        total[...] += jnp.sum(weight, axis=1, keepdims=True)
        numer[...] += jnp.dot(weight.astype(jnp.bfloat16), fbuf[b], preferred_element_type=jnp.float32)

    ready = False
    sims_rate = 2
    per_step = 4
    neighbour_sums(me, sims_ref[...], sq_ref[...])
    for step in range(1, n_fwd + 1):
        for direction in (0, 1):
            advance("f", direction)
        if state["s"][0] < count[0] or state["s"][1] < count[1]:
            for _ in range(sims_rate):
                for direction in (0, 1):
                    advance("s", direction)
        elif not ready:
            share_widths()
            ready = True
        if ready:
            for _ in range(per_step):
                if pending:
                    process(pending.pop(0))
    for direction in (0, 1):
        finish("f", direction)
    if not ready:
        share_widths()
    for b in pending:
        process(b)
    for c in copies + wid:
        c.wait_send()

    out_ref[...] = (numer[...] / total[...]).astype(out_ref.dtype)


def posterior(field, sims, sq, obs, nbr, n_z, n_col):
    n = 4 * n_z
    n_fwd = n // 2
    rows = n_col * obs.shape[0]
    vmem = pltpu.VMEM
    return pl.pallas_call(
        functools.partial(posterior_kernel, n_z),
        out_shape=jax.ShapeDtypeStruct((rows, field.shape[1]), field.dtype),
        in_specs=[pl.BlockSpec(memory_space=vmem)] * 5,
        out_specs=pl.BlockSpec(memory_space=vmem),
        scratch_shapes=[
            vmem((n,) + field.shape, field.dtype),
            vmem((n,) + sims.shape, sims.dtype),
            vmem((n,) + sq.shape, sq.dtype),
            vmem((n_col,) + obs.shape, obs.dtype),
            vmem((n_col, obs.shape[0], 1), jnp.float32),
            vmem((rows, field.shape[1]), jnp.float32),
            vmem((rows, 1), jnp.float32),
            vmem((obs.shape[0], 1), jnp.float32),
            vmem((rows, 1), jnp.float32),
            vmem((rows, 1), jnp.float32),
            pltpu.SemaphoreType.DMA((2, 3, n_fwd)),
            pltpu.SemaphoreType.DMA((2, 3, n_fwd)),
            pltpu.SemaphoreType.DMA((n_col - 1,)),
            pltpu.SemaphoreType.DMA((n_col,)),
            pltpu.SemaphoreType.DMA((n_col - 1,)),
            pltpu.SemaphoreType.DMA((n_col,)),
        ],
        compiler_params=pltpu.CompilerParams(
            collective_id=0, has_side_effects=True, vmem_limit_bytes=60 * 1024 * 1024
        ),
    )(field, sims, sq, obs, nbr)


def per_device(n_z, obs_summaries, sim_summaries, neighbours, field):
    n_col = 2 * lax.psum(1, "x")
    sim_float = sim_summaries.astype(jnp.float32)
    sim_square = jnp.sum(sim_float * sim_float, axis=1).reshape(1, -1)
    return posterior(field, sim_summaries, sim_square, obs_summaries, neighbours, n_z, n_col)


def solution(mesh):
    n_row, n_col = mesh.devices.shape
    n_z = n_row // 4
    fine = Mesh(mesh.devices.reshape(n_z, 2, 2, 2, n_col // 2), ROWS + COLS)
    return jax.shard_map(
        functools.partial(per_device, n_z),
        mesh=fine,
        in_specs=(
            P(ROWS + COLS, None),
            P(ROWS, None),
            P(ROWS + COLS, None),
            P(ROWS, COLS),
        ),
        out_specs=P(ROWS, COLS),
        check_vma=False,
    )
```

```python
import functools

import jax
import jax.numpy as jnp
from jax import lax
from jax.experimental import pallas as pl
from jax.experimental.pallas import tpu as pltpu
from jax.sharding import Mesh
from jax.sharding import PartitionSpec as P

SHARPNESS = 32.0
EPSILON = 1e-06
ROWS = ("z", "yh", "core")
COLS = ("yl", "x")
MESH = pl.DeviceIdType.MESH


def ring_device(pos, n_z, lane):
    chip = pos // 2
    core = pos % 2
    start = lane * (n_z // 2)
    low = chip < n_z
    z = jnp.where(low, (start + chip) % n_z, (start + 2 * n_z - 1 - chip) % n_z)
    yh = jnp.where(low, 0, 1)
    return z, yh, core


def posterior_kernel(
    n_z, field_ref, sims_ref, sq_ref, obs_ref, nbr_ref, out_ref,
    fbuf, sbuf, qbuf, obuf, wbuf, numer, wbig, total, ns,
    send_sem, recv_sem, col_send, col_recv, wid_send, wid_recv,
):
    z = lax.axis_index("z")
    yh = lax.axis_index("yh")
    core = lax.axis_index("core")
    yl = lax.axis_index("yl")
    x = lax.axis_index("x")
    n = 4 * n_z
    n_col = obuf.shape[0]
    n_x = n_col // 2
    sim_dev = sims_ref.shape[0]
    start = yl * (n_z // 2)
    rel = (z - start + n_z) % n_z
    chip = jnp.where(yh == 0, rel, 2 * n_z - 1 - rel)
    pos = 2 * chip + core
    me = (z * 2 + yh) * 2 + core
    mine = yl * n_x + x
    peers = [(mine + d) % n_col for d in range(1, n_col)]
    peer_devs = [(z, yh, core, p // n_x, p % n_x) for p in peers]

    def dev(p):
        dz, dyh, dcore = ring_device(p, n_z, yl)
        return (dz, dyh, dcore, yl, x)

    def origin(p):
        dz, dyh, dcore = ring_device(p, n_z, yl)
        return (dz * 2 + dyh) * 2 + dcore

    right = dev((pos + 1) % n)
    left = dev((pos + n - 1) % n)

    barrier = pltpu.get_barrier_semaphore()
    for d in [left, right] + peer_devs:
        pl.semaphore_signal(barrier, inc=1, device_id=d, device_id_type=MESH)
    pl.semaphore_wait(barrier, 2 + len(peer_devs))

    copies = []
    for i, d in enumerate(peer_devs):
        c = pltpu.make_async_remote_copy(
            src_ref=obs_ref, dst_ref=obuf.at[mine], send_sem=col_send.at[i],
            recv_sem=col_recv.at[mine], device_id=d, device_id_type=MESH,
        )
        c.start()
        copies.append(c)

    n_fwd = n // 2
    n_bwd = n - 1 - n_fwd
    pairs = ((field_ref, fbuf), (sims_ref, sbuf), (sq_ref, qbuf))

    def block(buf, o):
        if buf is fbuf:
            return fbuf.at[pl.ds(pl.multiple_of(o * sim_dev, sim_dev), sim_dev)]
        return buf.at[o]

    def hop(direction, step, target):
        if direction == 0:
            src_pos = (pos - step + 1 + n) % n
        else:
            src_pos = (pos + step - 1) % n
        o = origin(src_pos)
        made = []
        for k, (src_in, buf) in enumerate(pairs):
            src = src_in if step == 1 else block(buf, o)
            made.append(
                pltpu.make_async_remote_copy(
                    src_ref=src, dst_ref=block(buf, o),
                    send_sem=send_sem.at[direction, k, step - 1],
                    recv_sem=recv_sem.at[direction, k, step - 1],
                    device_id=target, device_id_type=MESH,
                )
            )
        return made

    obs_own = obs_ref[...]
    obs_own_f = obs_own.astype(jnp.float32)
    obs_own_sq = jnp.sum(obs_own_f * obs_own_f, axis=1, keepdims=True)
    nbr = nbr_ref[...]
    ns[...] = jnp.zeros_like(ns)

    def neighbour_sums(o, sims_blk, sq_blk):
        cross = lax.dot_general(
            obs_own, sims_blk, (((1,), (1,)), ((), ())), preferred_element_type=jnp.float32
        )
        dist = obs_own_sq + sq_blk - 2.0 * cross
        ids = lax.broadcasted_iota(jnp.int32, dist.shape, 1) + o * sim_dev
        counts = jnp.zeros(dist.shape, jnp.float32)
        for k in range(nbr.shape[1]):
            counts = counts + (nbr[:, k : k + 1] == ids).astype(jnp.float32)
        ns[...] += jnp.sum(counts * dist, axis=1, keepdims=True)

    fbuf[pl.ds(pl.multiple_of(me * sim_dev, sim_dev), sim_dev)] = field_ref[...]
    sbuf[me] = sims_ref[...]
    qbuf[me] = sq_ref[...]
    obuf[mine] = obs_own

    prev = {0: None, 1: None}
    for step in range(1, n_fwd + 1):
        arrived = []
        for direction, count, target in ((0, n_fwd, right), (1, n_bwd, left)):
            if step > count:
                continue
            if prev[direction] is not None:
                for c in prev[direction]:
                    c.wait_recv()
                arrived.append(direction)
            made = hop(direction, step, target)
            for c in made:
                c.start()
            copies.extend(made)
            prev[direction] = made
        if step == 1:
            neighbour_sums(me, sims_ref[...], sq_ref[...])
        for direction in arrived:
            got = (pos - step + 1 + n) % n if direction == 0 else (pos + step - 1) % n
            o = origin(got)
            neighbour_sums(o, sbuf[o], qbuf[o])
    for direction, count in ((0, n_fwd), (1, n_bwd)):
        for c in prev[direction]:
            c.wait_recv()
        got = (pos - count + n) % n if direction == 0 else (pos + count) % n
        o = origin(got)
        neighbour_sums(o, sbuf[o], qbuf[o])

    wbuf[mine] = ns[...] / nbr.shape[1] + EPSILON
    wid = []
    for i, d in enumerate(peer_devs):
        c = pltpu.make_async_remote_copy(
            src_ref=wbuf.at[mine], dst_ref=wbuf.at[mine], send_sem=wid_send.at[i],
            recv_sem=wid_recv.at[mine], device_id=d, device_id_type=MESH,
        )
        c.start()
        wid.append(c)
    for p in peers:
        pltpu.make_async_remote_copy(
            src_ref=obuf.at[p], dst_ref=obuf.at[p], send_sem=col_send.at[0],
            recv_sem=col_recv.at[p], device_id=peer_devs[0], device_id_type=MESH,
        ).wait_recv()
        pltpu.make_async_remote_copy(
            src_ref=wbuf.at[p], dst_ref=wbuf.at[p], send_sem=wid_send.at[0],
            recv_sem=wid_recv.at[p], device_id=peer_devs[0], device_id_type=MESH,
        ).wait_recv()
    for c in copies + wid:
        c.wait_send()

    rows = n_col * obs_ref.shape[0]
    obs_all = obuf[...].reshape(rows, obs_ref.shape[1])
    obs_all_f = obs_all.astype(jnp.float32)
    obs_sq = jnp.sum(obs_all_f * obs_all_f, axis=1, keepdims=True)
    width = wbuf[...].reshape(rows, 1)
    total[...] = jnp.zeros_like(total)
    scale = -SHARPNESS / width

    @pl.loop(0, n)
    def _(b):
        cross = lax.dot_general(
            obs_all, sbuf[b], (((1,), (1,)), ((), ())), preferred_element_type=jnp.float32
        )
        dist = obs_sq + qbuf[b] - 2.0 * cross
        weight = jnp.exp(dist * scale)
        total[...] += jnp.sum(weight, axis=1, keepdims=True)
        wbig[:, pl.ds(pl.multiple_of(b * sim_dev, sim_dev), sim_dev)] = weight.astype(jnp.bfloat16)

    cols = numer.shape[1]
    step = 256
    for j in range(cols // step):
        part = jnp.dot(wbig[...], fbuf[:, pl.ds(j * step, step)], preferred_element_type=jnp.float32)
        out_ref[:, pl.ds(j * step, step)] = (part / total[...]).astype(out_ref.dtype)


def posterior(field, sims, sq, obs, nbr, n_z, n_col):
    n = 4 * n_z
    n_fwd = n // 2
    rows = n_col * obs.shape[0]
    vmem = pltpu.VMEM
    return pl.pallas_call(
        functools.partial(posterior_kernel, n_z),
        out_shape=jax.ShapeDtypeStruct((rows, field.shape[1]), field.dtype),
        in_specs=[pl.BlockSpec(memory_space=vmem)] * 5,
        out_specs=pl.BlockSpec(memory_space=vmem),
        scratch_shapes=[
            vmem((n * field.shape[0], field.shape[1]), field.dtype),
            vmem((n,) + sims.shape, sims.dtype),
            vmem((n,) + sq.shape, sq.dtype),
            vmem((n_col,) + obs.shape, obs.dtype),
            vmem((n_col, obs.shape[0], 1), jnp.float32),
            vmem((rows, field.shape[1]), jnp.float32),
            vmem((rows, n * field.shape[0]), jnp.bfloat16),
            vmem((rows, 1), jnp.float32),
            vmem((obs.shape[0], 1), jnp.float32),
            pltpu.SemaphoreType.DMA((2, 3, n_fwd)),
            pltpu.SemaphoreType.DMA((2, 3, n_fwd)),
            pltpu.SemaphoreType.DMA((n_col - 1,)),
            pltpu.SemaphoreType.DMA((n_col,)),
            pltpu.SemaphoreType.DMA((n_col - 1,)),
            pltpu.SemaphoreType.DMA((n_col,)),
        ],
        compiler_params=pltpu.CompilerParams(
            collective_id=0, has_side_effects=True, vmem_limit_bytes=60 * 1024 * 1024
        ),
    )(field, sims, sq, obs, nbr)


def per_device(n_z, obs_summaries, sim_summaries, neighbours, field):
    n_col = 2 * lax.psum(1, "x")
    sim_float = sim_summaries.astype(jnp.float32)
    sim_square = jnp.sum(sim_float * sim_float, axis=1).reshape(1, -1)
    return posterior(field, sim_summaries, sim_square, obs_summaries, neighbours, n_z, n_col)


def solution(mesh):
    n_row, n_col = mesh.devices.shape
    n_z = n_row // 4
    fine = Mesh(mesh.devices.reshape(n_z, 2, 2, 2, n_col // 2), ROWS + COLS)
    return jax.shard_map(
        functools.partial(per_device, n_z),
        mesh=fine,
        in_specs=(
            P(ROWS + COLS, None),
            P(ROWS, None),
            P(ROWS + COLS, None),
            P(ROWS, COLS),
        ),
        out_specs=P(ROWS, COLS),
        check_vma=False,
    )
```

```python
import functools

import jax
import jax.numpy as jnp
from jax import lax
from jax.experimental import pallas as pl
from jax.experimental.pallas import tpu as pltpu
from jax.sharding import Mesh
from jax.sharding import PartitionSpec as P

SHARPNESS = 32.0
EPSILON = 1e-06
ROWS = ("z", "yh", "core")
COLS = ("yl", "x")
MESH = pl.DeviceIdType.MESH


def ring_device(pos, n_z, lane):
    chip = pos // 2
    core = pos % 2
    start = lane * (n_z // 2)
    low = chip < n_z
    z = jnp.where(low, (start + chip) % n_z, (start + 2 * n_z - 1 - chip) % n_z)
    yh = jnp.where(low, 0, 1)
    return z, yh, core


def posterior_kernel(
    n_z, field_ref, sims_ref, sq_ref, obs_ref, nbr_ref, out_ref,
    fbuf, sbuf, qbuf, obuf, wbuf, dbig, wbig, total, ns, osq,
    send_sem, recv_sem, col_send, col_recv, wid_send, wid_recv,
):
    z = lax.axis_index("z")
    yh = lax.axis_index("yh")
    core = lax.axis_index("core")
    yl = lax.axis_index("yl")
    x = lax.axis_index("x")
    n = 4 * n_z
    n_col = obuf.shape[0]
    n_x = n_col // 2
    sim_dev = sims_ref.shape[0]
    start = yl * (n_z // 2)
    rel = (z - start + n_z) % n_z
    chip = jnp.where(yh == 0, rel, 2 * n_z - 1 - rel)
    pos = 2 * chip + core
    me = (z * 2 + yh) * 2 + core
    mine = yl * n_x + x
    peers = [(mine + d) % n_col for d in range(1, n_col)]
    peer_devs = [(z, yh, core, p // n_x, p % n_x) for p in peers]

    def dev(p):
        dz, dyh, dcore = ring_device(p, n_z, yl)
        return (dz, dyh, dcore, yl, x)

    def origin(p):
        dz, dyh, dcore = ring_device(p, n_z, yl)
        return (dz * 2 + dyh) * 2 + dcore

    right = dev((pos + 1) % n)
    left = dev((pos + n - 1) % n)

    barrier = pltpu.get_barrier_semaphore()
    for d in [left, right] + peer_devs:
        pl.semaphore_signal(barrier, inc=1, device_id=d, device_id_type=MESH)
    pl.semaphore_wait(barrier, 2 + len(peer_devs))

    copies = []
    for i, d in enumerate(peer_devs):
        c = pltpu.make_async_remote_copy(
            src_ref=obs_ref, dst_ref=obuf.at[mine], send_sem=col_send.at[i],
            recv_sem=col_recv.at[mine], device_id=d, device_id_type=MESH,
        )
        c.start()
        copies.append(c)

    n_fwd = n // 2
    n_bwd = n - 1 - n_fwd
    pairs = ((field_ref, fbuf), (sims_ref, sbuf), (sq_ref, qbuf))

    def block(buf, o):
        if buf is fbuf:
            return fbuf.at[pl.ds(pl.multiple_of(o * sim_dev, sim_dev), sim_dev)]
        return buf.at[o]

    def hop(direction, step, target):
        if direction == 0:
            src_pos = (pos - step + 1 + n) % n
        else:
            src_pos = (pos + step - 1) % n
        o = origin(src_pos)
        made = []
        for k, (src_in, buf) in enumerate(pairs):
            src = src_in if step == 1 else block(buf, o)
            made.append(
                pltpu.make_async_remote_copy(
                    src_ref=src, dst_ref=block(buf, o),
                    send_sem=send_sem.at[direction, k, step - 1],
                    recv_sem=recv_sem.at[direction, k, step - 1],
                    device_id=target, device_id_type=MESH,
                )
            )
        return made

    obs_own = obs_ref[...]
    obs_own_f = obs_own.astype(jnp.float32)
    obs_own_sq = jnp.sum(obs_own_f * obs_own_f, axis=1, keepdims=True)
    nbr = nbr_ref[...]
    ns[...] = jnp.zeros_like(ns)

    def neighbour_sums(o, sims_blk, sq_blk):
        cross = lax.dot_general(
            obs_own, sims_blk, (((1,), (1,)), ((), ())), preferred_element_type=jnp.float32
        )
        dist = obs_own_sq + sq_blk - 2.0 * cross
        ids = lax.broadcasted_iota(jnp.int32, dist.shape, 1) + o * sim_dev
        counts = jnp.zeros(dist.shape, jnp.float32)
        for k in range(nbr.shape[1]):
            counts = counts + (nbr[:, k : k + 1] == ids).astype(jnp.float32)
        ns[...] += jnp.sum(counts * dist, axis=1, keepdims=True)
        cross_all = lax.dot_general(
            obuf[...].reshape(rows, obs_ref.shape[1]), sims_blk, (((1,), (1,)), ((), ())),
            preferred_element_type=jnp.float32,
        )
        dbig[:, pl.ds(pl.multiple_of(o * sim_dev, sim_dev), sim_dev)] = osq[...] + sq_blk - 2.0 * cross_all

    rows = n_col * obs_ref.shape[0]
    fbuf[pl.ds(pl.multiple_of(me * sim_dev, sim_dev), sim_dev)] = field_ref[...]
    sbuf[me] = sims_ref[...]
    qbuf[me] = sq_ref[...]
    obuf[mine] = obs_own

    prev = {0: None, 1: None}
    for step in range(1, n_fwd + 1):
        arrived = []
        for direction, count, target in ((0, n_fwd, right), (1, n_bwd, left)):
            if step > count:
                continue
            if prev[direction] is not None:
                for c in prev[direction]:
                    c.wait_recv()
                arrived.append(direction)
            made = hop(direction, step, target)
            for c in made:
                c.start()
            copies.extend(made)
            prev[direction] = made
        if step == 1:
            for p in peers:
                pltpu.make_async_remote_copy(
                    src_ref=obuf.at[p], dst_ref=obuf.at[p], send_sem=col_send.at[0],
                    recv_sem=col_recv.at[p], device_id=peer_devs[0], device_id_type=MESH,
                ).wait_recv()
            obs_all_f = obuf[...].reshape(rows, obs_ref.shape[1]).astype(jnp.float32)
            osq[...] = jnp.sum(obs_all_f * obs_all_f, axis=1, keepdims=True)
            neighbour_sums(me, sims_ref[...], sq_ref[...])
        for direction in arrived:
            got = (pos - step + 1 + n) % n if direction == 0 else (pos + step - 1) % n
            o = origin(got)
            neighbour_sums(o, sbuf[o], qbuf[o])
    for direction, count in ((0, n_fwd), (1, n_bwd)):
        for c in prev[direction]:
            c.wait_recv()
        got = (pos - count + n) % n if direction == 0 else (pos + count) % n
        o = origin(got)
        neighbour_sums(o, sbuf[o], qbuf[o])

    wbuf[mine] = ns[...] / nbr.shape[1] + EPSILON
    wid = []
    for i, d in enumerate(peer_devs):
        c = pltpu.make_async_remote_copy(
            src_ref=wbuf.at[mine], dst_ref=wbuf.at[mine], send_sem=wid_send.at[i],
            recv_sem=wid_recv.at[mine], device_id=d, device_id_type=MESH,
        )
        c.start()
        wid.append(c)
    for p in peers:
        pltpu.make_async_remote_copy(
            src_ref=wbuf.at[p], dst_ref=wbuf.at[p], send_sem=wid_send.at[0],
            recv_sem=wid_recv.at[p], device_id=peer_devs[0], device_id_type=MESH,
        ).wait_recv()
    for c in copies + wid:
        c.wait_send()

    width = wbuf[...].reshape(rows, 1)
    total[...] = jnp.zeros_like(total)
    scale = -SHARPNESS / width

    @pl.loop(0, n)
    def _(b):
        dist = dbig[:, pl.ds(pl.multiple_of(b * sim_dev, sim_dev), sim_dev)]
        weight = jnp.exp(dist * scale)
        total[...] += jnp.sum(weight, axis=1, keepdims=True)
        wbig[:, pl.ds(pl.multiple_of(b * sim_dev, sim_dev), sim_dev)] = weight.astype(jnp.bfloat16)

    cols = out_ref.shape[1]
    step = 256
    for j in range(cols // step):
        part = jnp.dot(wbig[...], fbuf[:, pl.ds(j * step, step)], preferred_element_type=jnp.float32)
        out_ref[:, pl.ds(j * step, step)] = (part / total[...]).astype(out_ref.dtype)


def posterior(field, sims, sq, obs, nbr, n_z, n_col):
    n = 4 * n_z
    n_fwd = n // 2
    rows = n_col * obs.shape[0]
    vmem = pltpu.VMEM
    return pl.pallas_call(
        functools.partial(posterior_kernel, n_z),
        out_shape=jax.ShapeDtypeStruct((rows, field.shape[1]), field.dtype),
        in_specs=[pl.BlockSpec(memory_space=vmem)] * 5,
        out_specs=pl.BlockSpec(memory_space=vmem),
        scratch_shapes=[
            vmem((n * field.shape[0], field.shape[1]), field.dtype),
            vmem((n,) + sims.shape, sims.dtype),
            vmem((n,) + sq.shape, sq.dtype),
            vmem((n_col,) + obs.shape, obs.dtype),
            vmem((n_col, obs.shape[0], 1), jnp.float32),
            vmem((rows, n * field.shape[0]), jnp.float32),
            vmem((rows, n * field.shape[0]), jnp.bfloat16),
            vmem((rows, 1), jnp.float32),
            vmem((obs.shape[0], 1), jnp.float32),
            vmem((rows, 1), jnp.float32),
            pltpu.SemaphoreType.DMA((2, 3, n_fwd)),
            pltpu.SemaphoreType.DMA((2, 3, n_fwd)),
            pltpu.SemaphoreType.DMA((n_col - 1,)),
            pltpu.SemaphoreType.DMA((n_col,)),
            pltpu.SemaphoreType.DMA((n_col - 1,)),
            pltpu.SemaphoreType.DMA((n_col,)),
        ],
        compiler_params=pltpu.CompilerParams(
            collective_id=0, has_side_effects=True, vmem_limit_bytes=60 * 1024 * 1024
        ),
    )(field, sims, sq, obs, nbr)


def per_device(n_z, obs_summaries, sim_summaries, neighbours, field):
    n_col = 2 * lax.psum(1, "x")
    sim_float = sim_summaries.astype(jnp.float32)
    sim_square = jnp.sum(sim_float * sim_float, axis=1).reshape(1, -1)
    return posterior(field, sim_summaries, sim_square, obs_summaries, neighbours, n_z, n_col)


def solution(mesh):
    n_row, n_col = mesh.devices.shape
    n_z = n_row // 4
    fine = Mesh(mesh.devices.reshape(n_z, 2, 2, 2, n_col // 2), ROWS + COLS)
    return jax.shard_map(
        functools.partial(per_device, n_z),
        mesh=fine,
        in_specs=(
            P(ROWS + COLS, None),
            P(ROWS, None),
            P(ROWS + COLS, None),
            P(ROWS, COLS),
        ),
        out_specs=P(ROWS, COLS),
        check_vma=False,
    )
```
